32 devices in a mesh: blk: 8 (over z, x), rep: 4 (over y, core).
Axes of the slice: x: 2, y: 2, z: 4, core: 2. Of those that a mesh axis runs over, the one named last changes fastest.
Arguments:
- features: bfloat16 [32768, 128], P('blk'), may hold values from -6 to 6
- weight: bfloat16 [128, 256], replicated, may hold values from -0.5 to 0.5
- bias: float32 [256], replicated, may hold values from -3 to 3
- tile_values: bfloat16 [8, 8, 160, 128, 128], P('blk', 'rep'), may hold values from 0 to 0.041748047
- tile_place: int32 [8, 8, 160], P('blk', 'rep'), may hold values from 0 to 1023, as said below
- tile_count: int32 [8, 8], P('blk', 'rep'), may hold values from 1 to 160, as said below
Outputs:
- activations: bfloat16 [32768, 256], P('blk')
The draws below stay inside these ranges and needn't reach their ends.
Inputs may be any that keep to these rules, and one draw needn't show every extreme that they name: `tile_place`: within one pair of destination block and section the 160 positions are distinct. `tile_count`: some pair of destination block and section has all 160 slots occupied.
All inputs are finite; a program needn't handle non-finite values.
Results may differ from the reference program's by a relative error of at most 0.0046.
Values may be sent and summed in bfloat16 or wider, within the bound.
A program may use at most 128 MiB of HBM per device.

```python
import jax
import jax.numpy as jnp
from jax import lax

F_IN = 128
HIDDEN_SIZE = 256
TILE = 128
ROWS_BLK = 4096
SLOTS = 160
BLOCKS = 8
NODES = 32768


def draw_tile_count(key, part):
    base = jax.random.fold_in(key, 11)
    first_key, second_key, third_key = jax.random.split(base, 3)
    first_draw = jax.random.randint(first_key, (BLOCKS * BLOCKS,), 1, SLOTS + 1)
    second_draw = jax.random.randint(second_key, (BLOCKS * BLOCKS,), 1, SLOTS + 1)
    counts = jnp.minimum(first_draw, second_draw)
    chosen = jax.random.randint(third_key, (), 0, BLOCKS * BLOCKS)
    counts = jnp.where(jnp.arange(BLOCKS * BLOCKS, dtype=jnp.int32) == chosen, SLOTS, counts)
    return counts.reshape(BLOCKS, BLOCKS).astype(jnp.int32)


def draw_tile_place(key, part):
    base = jax.random.fold_in(key, 23)
    positions = ROWS_BLK // TILE * (ROWS_BLK // TILE)
    scores = jax.random.randint(base, (BLOCKS, BLOCKS, positions), 0, 2 ** 30 // positions)
    scores = scores * positions + jnp.arange(positions, dtype=jnp.int32)
    order = jnp.argsort(scores, axis=-1)
    return order[:, :, :SLOTS].astype(jnp.int32)


def block_scale(key, extent, shards, smallest, top_value):
    def one(dim, blocks):
        steps = jax.random.uniform(jax.random.fold_in(jax.random.fold_in(key, 6), dim), (blocks,), jnp.float32, smallest / len(shards), top_value / len(shards))
        return jnp.repeat(jnp.exp(steps), extent[dim] // blocks).reshape((-1,) + (1,) * (len(extent) - dim - 1))

    level = one(*shards[0])
    for cut in shards[1:]:
        level = level * one(*cut)
    return level


def centred(key, shape, spread, most, shards=(), kind=jnp.bfloat16):
    gain = block_scale(key, shape, shards, -0.22, 0.18) if shards else 1.0
    values = jax.random.normal(key, shape, jnp.float32) * spread * gain
    return jnp.minimum(jnp.maximum(values, -most), most).astype(kind)


def setup_inputs(seed: int = 0) -> dict:
    arg_keys = jax.random.split(jax.random.key(seed), 7)
    return {
        "features": centred(arg_keys[0], (NODES, F_IN), 1.0, 6.0, ((0, 8),)),
        "weight": centred(arg_keys[1], (F_IN, HIDDEN_SIZE), F_IN ** -0.5, 0.5),
        "bias": centred(arg_keys[2], (HIDDEN_SIZE,), 0.5, 3.0, (), jnp.float32),
        "tile_values": jnp.clip(0.041748047 * jax.random.uniform(arg_keys[3], (BLOCKS, BLOCKS, SLOTS, TILE, TILE), jnp.float32) ** block_scale(arg_keys[3], (BLOCKS, BLOCKS, SLOTS, TILE, TILE), ((0, 8), (1, 4)), -0.2, 0.2), 0.0, 0.041748047).astype(jnp.bfloat16),
        "tile_place": draw_tile_place(jax.random.fold_in(arg_keys[6], 71), 0),
        "tile_count": draw_tile_count(jax.random.fold_in(arg_keys[6], 71), 0),
    }


def reference(features, weight, bias, tile_values, tile_place, tile_count):
    row_tiles = ROWS_BLK // TILE
    blocked = features.reshape(BLOCKS, row_tiles, TILE, F_IN)
    section_ids = jnp.arange(BLOCKS, dtype=jnp.int32)
    slot_ids = jnp.arange(SLOTS, dtype=jnp.int32)
    tile_rows = jnp.arange(row_tiles, dtype=jnp.int32)

    def one_block(dest):
        sources = ((dest - section_ids) % BLOCKS).astype(jnp.int32)
        place = tile_place[dest]
        column = place % row_tiles
        target = place // row_tiles
        pieces = blocked[sources[:, None], column]
        products = jnp.einsum("skij,skjf->skif", tile_values[dest].astype(jnp.float32), pieces.astype(jnp.float32))
        live = (slot_ids[None, :] < tile_count[dest][:, None]).astype(jnp.float32)
        picker = (target[:, :, None] == tile_rows[None, None, :]).astype(jnp.float32) * live[:, :, None]
        summed = jnp.einsum("skr,skif->rif", picker, products, precision=lax.Precision.HIGHEST)
        return summed.reshape(ROWS_BLK, F_IN)

    summed = lax.map(one_block, jnp.arange(BLOCKS, dtype=jnp.int32)).reshape(NODES, F_IN)
    aggregated = summed.astype(jnp.bfloat16)
    output = jnp.dot(aggregated, weight, preferred_element_type=jnp.float32) + bias
    return jnp.maximum(output, 0.0).astype(jnp.bfloat16)
```

```python
import functools

import jax
import jax.numpy as jnp
from jax import lax
from jax.experimental import pallas as pl
from jax.experimental.pallas import tpu as pltpu
from jax.sharding import PartitionSpec as P

MESH = pl.DeviceIdType.MESH
GROUP = 8
BLOCK = 32
CHUNKS = 4


def largest_divisor(number, most):
    return max(d for d in range(1, most + 1) if number % d == 0)


def section_kernel(first, group, place_ref, count_ref, source_ref, tiles_ref, *rest):
    acc_in_ref, acc_ref = (None, rest[0]) if first else rest
    step = pl.program_id(0)
    slots, tile = tiles_ref.shape[2], tiles_ref.shape[3]
    row_tiles = source_ref.shape[0] // tile
    count = count_ref[0]
    base = step * slots

    @pl.when(step == 0)
    def _():
        acc_ref[...] = jnp.zeros_like(acc_ref) if first else acc_in_ref[...]

    def body(g, carry):
        products, targets = [], []
        for u in range(group):
            k = g * group + u
            place = place_ref[base + k]
            column = lax.rem(place, row_tiles)
            targets.append(lax.div(place, row_tiles))
            piece = source_ref[pl.ds(pl.multiple_of(column * tile, tile), tile), :]
            product = jnp.dot(tiles_ref[0, 0, k], piece, preferred_element_type=jnp.float32)
            products.append(jnp.where(base + k < count, product, 0.0))
        for target, product in zip(targets, products):
            rows = pl.ds(pl.multiple_of(target * tile, tile), tile)
            acc_ref[rows, :] += product
        return carry

    live = jnp.clip(count - base, 0, slots)
    lax.fori_loop(0, (live + group - 1) // group, body, 0)


def section_sum(acc, source, tile_values, place, count, section):
    slots, tile = tile_values.shape[2], tile_values.shape[3]
    rows, width = source.shape
    block = largest_divisor(slots, BLOCK)
    group = largest_divisor(block, GROUP)
    first = acc is None

    def tiles_map(step, place_ref, count_ref):
        return (0, section, jnp.minimum(step, jnp.maximum(count_ref[0] - 1, 0) // block), 0, 0)

    whole = pl.BlockSpec((rows, width), lambda step, *_: (0, 0))
    in_specs = [whole, pl.BlockSpec((1, 1, block, tile, tile), tiles_map)]
    args = [source, tile_values]
    if not first:
        in_specs.append(whole)
        args.append(acc)
    return pl.pallas_call(
        functools.partial(section_kernel, first, group),
        out_shape=jax.ShapeDtypeStruct((rows, width), jnp.float32),
        grid_spec=pltpu.PrefetchScalarGridSpec(
            num_scalar_prefetch=2, grid=(slots // block,), in_specs=in_specs, out_specs=whole
        ),
        cost_estimate=pl.CostEstimate(
            flops=2 * slots * tile * tile * width, bytes_accessed=slots * tile * tile * 2, transcendentals=0
        ),
        name="section_sum",
    )(place, count, *args)


def reduce_kernel(chips, chunks, part_ref, agg_ref, core_in, send_buf, recv_buf,
                  s1, r1, s2, r2, s3, r3, s4, r4):
    blk, rep = lax.axis_index("blk"), lax.axis_index("rep")
    core, chip = lax.rem(rep, 2), lax.div(rep, 2)
    rows = part_ref.shape[0]
    half = rows // 2
    size = half // chips // chunks
    other = chip * 2 + (1 - core)

    def peer(d):
        return lax.rem(chip + d, chips)

    def local(piece, ch):
        return pl.ds(pl.multiple_of((piece * chunks + ch) * size, size), size)

    def place(which, piece, ch):
        return pl.ds(pl.multiple_of(which * half + (piece * chunks + ch) * size, size), size)

    barrier = pltpu.get_barrier_semaphore()
    pl.semaphore_signal(barrier, inc=1, device_id=(blk, other), device_id_type=MESH)
    for d in range(1, chips):
        pl.semaphore_signal(barrier, inc=1, device_id=(blk, peer(d) * 2 + core), device_id_type=MESH)
    pl.semaphore_wait(barrier, chips)

    order = [(ch, d) for ch in range(chunks) for d in list(range(1, chips)) + [0]]
    stage1, stage2, stage3, stage4 = {}, {}, {}, {}
    for ch, d in order:
        copy = pltpu.make_async_remote_copy(
            src_ref=part_ref.at[place(1 - core, peer(d), ch)], dst_ref=core_in.at[local(peer(d), ch)],
            send_sem=s1.at[d, ch], recv_sem=r1.at[d, ch], device_id=(blk, other), device_id_type=MESH)
        copy.start()
        stage1[ch, d] = copy
    for ch, d in order:
        if d == 0:
            continue
        stage1[ch, d].wait_recv()
        total = part_ref[place(core, peer(d), ch), :] + core_in[local(peer(d), ch), :]
        send_buf[d - 1, ch] = total.astype(jnp.bfloat16)
        copy = pltpu.make_async_remote_copy(
            src_ref=send_buf.at[d - 1, ch], dst_ref=recv_buf.at[d - 1, ch],
            send_sem=s2.at[d, ch], recv_sem=r2.at[d, ch],
            device_id=(blk, peer(d) * 2 + core), device_id_type=MESH)
        copy.start()
        stage2[ch, d] = copy
    for ch in range(chunks):
        stage1[ch, 0].wait_recv()
        total = part_ref[place(core, chip, ch), :] + core_in[local(chip, ch), :]
        for d in range(1, chips):
            stage2[ch, d].wait_recv()
            total = total + recv_buf[d - 1, ch].astype(jnp.float32)
        mine = place(core, chip, ch)
        agg_ref[mine, :] = total.astype(jnp.bfloat16)
        for d in list(range(1, chips)) + [0]:
            target = other if d == 0 else peer(d) * 2 + core
            copy = pltpu.make_async_remote_copy(
                src_ref=agg_ref.at[mine], dst_ref=agg_ref.at[mine],
                send_sem=s3.at[d, ch], recv_sem=r3.at[d, ch],
                device_id=(blk, target), device_id_type=MESH)
            copy.start()
            stage3[ch, d] = copy
    for ch in range(chunks):
        for d in range(1, chips):
            stage3[ch, d].wait_recv()
            came = place(core, lax.rem(chip + chips - d, chips), ch)
            copy = pltpu.make_async_remote_copy(
                src_ref=agg_ref.at[came], dst_ref=agg_ref.at[came],
                send_sem=s4.at[d, ch], recv_sem=r4.at[d, ch],
                device_id=(blk, other), device_id_type=MESH)
            copy.start()
            stage4[ch, d] = copy
    for ch, d in order:
        stage1[ch, d].wait_send()
        stage3[ch, d].wait_send()
        if d == 0:
            stage3[ch, d].wait_recv()
        else:
            stage2[ch, d].wait_send()
            stage4[ch, d].wait()


def replica_sum(part, replicas):
    rows, width = part.shape
    chips = replicas // 2
    chunks = largest_divisor(rows // 2 // chips // 16, CHUNKS)
    size = rows // 2 // chips // chunks
    dma = pltpu.SemaphoreType.DMA((chips, chunks))
    vmem = pl.BlockSpec(memory_space=pltpu.VMEM)
    return pl.pallas_call(
        functools.partial(reduce_kernel, chips, chunks),
        out_shape=jax.ShapeDtypeStruct((rows, width), jnp.bfloat16),
        in_specs=[vmem],
        out_specs=vmem,
        scratch_shapes=[
            pltpu.VMEM((rows // 2, width), jnp.float32),
            pltpu.VMEM((chips - 1, chunks, size, width), jnp.bfloat16),
            pltpu.VMEM((chips - 1, chunks, size, width), jnp.bfloat16),
        ] + [dma] * 8,
        compiler_params=pltpu.CompilerParams(collective_id=0, has_side_effects=True),
        name="replica_sum",
    )(part)


def shards(blocks, replicas, features, weight, bias, tile_values, tile_place, tile_count):
    sections = tile_values.shape[1]
    sources = []
    for section in range(sections):
        pairs = [
            (b * replicas + r, (b + r * sections + section) % blocks * replicas + r)
            for b in range(blocks) for r in range(replicas)
        ]
        sources.append(lax.ppermute(features, ("blk", "rep"), pairs))
    part = None
    for section in range(sections):
        part = section_sum(part, sources[section], tile_values, tile_place[0, section],
                           tile_count[0, section][None], section)
    aggregated = replica_sum(part, replicas)
    output = jnp.dot(aggregated, weight, preferred_element_type=jnp.float32) + bias
    return jnp.maximum(output, 0.0).astype(jnp.bfloat16)


def solution(mesh):
    in_specs = (
        P("blk", None),
        P(),
        P(),
        P("blk", "rep", None, None, None),
        P("blk", "rep", None),
        P("blk", "rep"),
    )
    body = functools.partial(shards, mesh.shape["blk"], mesh.shape["rep"])
    return jax.shard_map(body, mesh=mesh, in_specs=in_specs, out_specs=P("blk", None), check_vma=False)
```

```python
import functools

import jax
import jax.numpy as jnp
from jax import lax
from jax.experimental import pallas as pl
from jax.experimental.pallas import tpu as pltpu
from jax.sharding import PartitionSpec as P

MESH = pl.DeviceIdType.MESH
GROUP = 8
BLOCK = 32
CHUNKS = 4


def largest_divisor(number, most):
    return max(d for d in range(1, most + 1) if number % d == 0)


def gather_kernel(blocks, replicas, sections, features_ref, source_ref, ring,
                  ring_send, ring_recv, give_send, give_recv, own_sem):
    blk, rep = lax.axis_index("blk"), lax.axis_index("rep")
    share = features_ref.shape[0] // replicas
    sub = share // 2
    odd = lax.rem(blk, 2)
    position = (1 - odd) * lax.div(blk, 2) + odd * (blocks - 1 - lax.div(blk, 2))

    def block_at(offset):
        p = lax.rem(position + blocks + offset, blocks)
        back = lax.div(p, blocks // 2)
        return (1 - back) * (2 * p) + back * (2 * (blocks - 1 - p) + 1)

    def rows(who, h):
        return pl.ds(pl.multiple_of(who * share + h * sub, sub), sub)

    hops = blocks // 2
    ways = (1, -1)
    barrier = pltpu.get_barrier_semaphore()
    for way in ways:
        pl.semaphore_signal(barrier, inc=1, device_id=(block_at(way), rep), device_id_type=MESH)
    for d in range(1, replicas):
        pl.semaphore_signal(barrier, inc=1, device_id=(blk, lax.rem(rep + d, replicas)), device_id_type=MESH)
    pl.semaphore_wait(barrier, replicas + 1)

    def ring_copy(w, k, h):
        source = features_ref.at[rows(rep, h)] if k == 0 else ring.at[w, k - 1, h]
        return pltpu.make_async_remote_copy(
            src_ref=source, dst_ref=ring.at[w, k, h], send_sem=ring_send.at[w, k, h],
            recv_sem=ring_recv.at[w, k, h], device_id=(block_at(ways[w]), rep), device_id_type=MESH)

    def travels(w, k, h):
        return k < hops - 1 or (k == hops - 1 and h == w)

    for h in range(2):
        for w in range(2):
            if travels(w, 0, h):
                ring_copy(w, 0, h).start()
    own = pltpu.make_async_copy(features_ref, source_ref.at[0], own_sem)

    @pl.when(rep == 0)
    def _():
        own.start()

    arrivals = [(k, h, w) for k in range(hops) for h in range(2) for w in range(2) if travels(w, k, h)]

    def give(k, h, w):
        section = lax.rem(blk - block_at(-ways[w] * (k + 1)) + blocks, blocks)
        target, index = lax.div(section, sections), lax.rem(section, sections)
        place = source_ref.at[index, rows(rep, h)]
        here = pltpu.make_async_copy(ring.at[w, k, h], place, give_send.at[w, k, h])
        there = pltpu.make_async_remote_copy(
            src_ref=ring.at[w, k, h], dst_ref=place, send_sem=give_send.at[w, k, h],
            recv_sem=give_recv.at[index, rep, h], device_id=(blk, target), device_id_type=MESH)
        return target, here, there

    for k, h, w in arrivals:
        ring_copy(w, k, h).wait_recv()
        if travels(w, k + 1, h):
            ring_copy(w, k + 1, h).start()
        target, here, there = give(k, h, w)

        @pl.when(target == rep)
        def _():
            here.start()

        @pl.when(target != rep)
        def _():
            there.start()

    for k, h, w in arrivals:
        ring_copy(w, k, h).wait_send()
        target, here, there = give(k, h, w)

        @pl.when(target == rep)
        def _():
            here.wait()

        @pl.when(target != rep)
        def _():
            there.wait_send()

    @pl.when(rep == 0)
    def _():
        own.wait()

    for index in range(sections):
        def arrive(index=index):
            for d in range(1, replicas):
                giver = lax.rem(rep + d, replicas)
                for h in range(2):
                    pltpu.make_async_remote_copy(
                        src_ref=ring.at[0, 0, h], dst_ref=source_ref.at[index, rows(giver, h)],
                        send_sem=give_send.at[0, 0, h], recv_sem=give_recv.at[index, giver, h],
                        device_id=(blk, giver), device_id_type=MESH).wait_recv()

        if index == 0:
            pl.when(rep != 0)(arrive)
        else:
            arrive()


def gather_sources(features, blocks, replicas, sections):
    rows, width = features.shape
    sub = rows // replicas // 2
    hops = blocks // 2
    vmem = pl.BlockSpec(memory_space=pltpu.VMEM)
    dma = pltpu.SemaphoreType.DMA
    return pl.pallas_call(
        functools.partial(gather_kernel, blocks, replicas, sections),
        out_shape=jax.ShapeDtypeStruct((sections, rows, width), features.dtype),
        in_specs=[vmem],
        out_specs=vmem,
        scratch_shapes=[
            pltpu.VMEM((2, hops, 2, sub, width), features.dtype),
            dma((2, hops, 2)), dma((2, hops, 2)), dma((2, hops, 2)), dma((sections, replicas, 2)), dma(()),
        ],
        compiler_params=pltpu.CompilerParams(collective_id=1, has_side_effects=True),
        name="gather_sources",
    )(features)


def sections_kernel(find, group, place_ref, count_ref, source_ref, tiles_ref, acc_ref):
    step = pl.program_id(0)
    slots, tile = tiles_ref.shape[2], tiles_ref.shape[3]
    row_tiles = source_ref.shape[1] // tile
    section, chunk, active = find(step, count_ref)
    count = count_ref[0, section]
    base = chunk * slots

    @pl.when(step == 0)
    def _():
        acc_ref[...] = jnp.zeros_like(acc_ref)

    def body(g, carry):
        products, targets = [], []
        for u in range(group):
            k = g * group + u
            place = place_ref[0, section, base + k]
            column = lax.rem(place, row_tiles)
            targets.append(lax.div(place, row_tiles))
            piece = source_ref[section, pl.ds(pl.multiple_of(column * tile, tile), tile), :]
            product = jnp.dot(tiles_ref[0, 0, k], piece, preferred_element_type=jnp.float32)
            products.append(jnp.where(base + k < count, product, 0.0))
        for target, product in zip(targets, products):
            rows = pl.ds(pl.multiple_of(target * tile, tile), tile)
            acc_ref[rows, :] += product
        return carry

    live = jnp.where(active, jnp.clip(count - base, 0, slots), 0)
    lax.fori_loop(0, (live + group - 1) // group, body, 0)


def section_sums(sources, tile_values, tile_place, tile_count):
    sections, slots, tile = tile_values.shape[1:4]
    rows, width = sources.shape[1:]
    block = largest_divisor(slots, BLOCK)
    group = largest_divisor(block, GROUP)

    def find(step, count_ref):
        section, chunk = jnp.int32(0), jnp.int32(0)
        start, active = jnp.int32(0), False
        for s in range(sections):
            steps = lax.div(count_ref[0, s] + block - 1, block)
            inside = step >= start
            section = jnp.where(inside, s, section)
            chunk = jnp.where(inside, jnp.minimum(step - start, steps - 1), chunk)
            start = start + steps
        return section, chunk, step < start

    def tiles_map(step, place_ref, count_ref):
        section, chunk, _ = find(step, count_ref)
        return (0, section, chunk, 0, 0)

    vmem = pl.BlockSpec(memory_space=pltpu.VMEM)
    return pl.pallas_call(
        functools.partial(sections_kernel, find, group),
        out_shape=jax.ShapeDtypeStruct((rows, width), jnp.float32),
        grid_spec=pltpu.PrefetchScalarGridSpec(
            num_scalar_prefetch=2, grid=(sections * slots // block,),
            in_specs=[vmem, pl.BlockSpec((1, 1, block, tile, tile), tiles_map)], out_specs=vmem
        ),
        name="section_sums",
    )(tile_place, tile_count, sources, tile_values)


def reduce_kernel(chips, chunks, part_ref, agg_ref, core_in, send_buf, recv_buf,
                  s1, r1, s2, r2, s3, r3, s4, r4):
    blk, rep = lax.axis_index("blk"), lax.axis_index("rep")
    core, chip = lax.rem(rep, 2), lax.div(rep, 2)
    rows = part_ref.shape[0]
    half = rows // 2
    size = half // chips // chunks
    other = chip * 2 + (1 - core)

    def peer(d):
        return lax.rem(chip + d, chips)

    def local(piece, ch):
        return pl.ds(pl.multiple_of((piece * chunks + ch) * size, size), size)

    def place(which, piece, ch):
        return pl.ds(pl.multiple_of(which * half + (piece * chunks + ch) * size, size), size)

    barrier = pltpu.get_barrier_semaphore()
    pl.semaphore_signal(barrier, inc=1, device_id=(blk, other), device_id_type=MESH)
    for d in range(1, chips):
        pl.semaphore_signal(barrier, inc=1, device_id=(blk, peer(d) * 2 + core), device_id_type=MESH)
    pl.semaphore_wait(barrier, chips)

    order = [(ch, d) for ch in range(chunks) for d in list(range(1, chips)) + [0]]
    stage1, stage2, stage3, stage4 = {}, {}, {}, {}
    for ch, d in order:
        copy = pltpu.make_async_remote_copy(
            src_ref=part_ref.at[place(1 - core, peer(d), ch)], dst_ref=core_in.at[local(peer(d), ch)],
            send_sem=s1.at[d, ch], recv_sem=r1.at[d, ch], device_id=(blk, other), device_id_type=MESH)
        copy.start()
        stage1[ch, d] = copy
    for ch, d in order:
        if d == 0:
            continue
        stage1[ch, d].wait_recv()
        total = part_ref[place(core, peer(d), ch), :] + core_in[local(peer(d), ch), :]
        send_buf[d - 1, ch] = total.astype(jnp.bfloat16)
        copy = pltpu.make_async_remote_copy(
            src_ref=send_buf.at[d - 1, ch], dst_ref=recv_buf.at[d - 1, ch],
            send_sem=s2.at[d, ch], recv_sem=r2.at[d, ch],
            device_id=(blk, peer(d) * 2 + core), device_id_type=MESH)
        copy.start()
        stage2[ch, d] = copy
    for ch in range(chunks):
        stage1[ch, 0].wait_recv()
        total = part_ref[place(core, chip, ch), :] + core_in[local(chip, ch), :]
        for d in range(1, chips):
            stage2[ch, d].wait_recv()
            total = total + recv_buf[d - 1, ch].astype(jnp.float32)
        mine = place(core, chip, ch)
        agg_ref[mine, :] = total.astype(jnp.bfloat16)
        for d in list(range(1, chips)) + [0]:
            target = other if d == 0 else peer(d) * 2 + core
            copy = pltpu.make_async_remote_copy(
                src_ref=agg_ref.at[mine], dst_ref=agg_ref.at[mine],
                send_sem=s3.at[d, ch], recv_sem=r3.at[d, ch],
                device_id=(blk, target), device_id_type=MESH)
            copy.start()
            stage3[ch, d] = copy
    for ch in range(chunks):
        for d in range(1, chips):
            stage3[ch, d].wait_recv()
            came = place(core, lax.rem(chip + chips - d, chips), ch)
            copy = pltpu.make_async_remote_copy(
                src_ref=agg_ref.at[came], dst_ref=agg_ref.at[came],
                send_sem=s4.at[d, ch], recv_sem=r4.at[d, ch],
                device_id=(blk, other), device_id_type=MESH)
            copy.start()
            stage4[ch, d] = copy
    for ch, d in order:
        stage1[ch, d].wait_send()
        stage3[ch, d].wait_send()
        if d == 0:
            stage3[ch, d].wait_recv()
        else:
            stage2[ch, d].wait_send()
            stage4[ch, d].wait()


def replica_sum(part, replicas):
    rows, width = part.shape
    chips = replicas // 2
    chunks = largest_divisor(rows // 2 // chips // 16, CHUNKS)
    size = rows // 2 // chips // chunks
    dma = pltpu.SemaphoreType.DMA((chips, chunks))
    vmem = pl.BlockSpec(memory_space=pltpu.VMEM)
    return pl.pallas_call(
        functools.partial(reduce_kernel, chips, chunks),
        out_shape=jax.ShapeDtypeStruct((rows, width), jnp.bfloat16),
        in_specs=[vmem],
        out_specs=vmem,
        scratch_shapes=[
            pltpu.VMEM((rows // 2, width), jnp.float32),
            pltpu.VMEM((chips - 1, chunks, size, width), jnp.bfloat16),
            pltpu.VMEM((chips - 1, chunks, size, width), jnp.bfloat16),
        ] + [dma] * 8,
        compiler_params=pltpu.CompilerParams(collective_id=0, has_side_effects=True),
        name="replica_sum",
    )(part)


def shards(blocks, replicas, features, weight, bias, tile_values, tile_place, tile_count):
    sources = gather_sources(features, blocks, replicas, tile_values.shape[1])
    part = section_sums(sources, tile_values, tile_place, tile_count)
    aggregated = replica_sum(part, replicas)
    output = jnp.dot(aggregated, weight, preferred_element_type=jnp.float32) + bias
    return jnp.maximum(output, 0.0).astype(jnp.bfloat16)


def solution(mesh):
    in_specs = (
        P("blk", None),
        P(),
        P(),
        P("blk", "rep", None, None, None),
        P("blk", "rep", None),
        P("blk", "rep"),
    )
    body = functools.partial(shards, mesh.shape["blk"], mesh.shape["rep"])
    return jax.shard_map(body, mesh=mesh, in_specs=in_specs, out_specs=P("blk", None), check_vma=False)
```

```python
import functools

import jax
import jax.numpy as jnp
from jax import lax
from jax.experimental import pallas as pl
from jax.experimental.pallas import tpu as pltpu
from jax.sharding import PartitionSpec as P

MESH = pl.DeviceIdType.MESH
GROUP = 16
BLOCK = 80
CHUNKS = 4
SUBS = 4
ROWS_STEP = 4096
GRANT = 16 * 1024 * 1024


def largest_divisor(number, most):
    return max(d for d in range(1, most + 1) if number % d == 0)


def gather_kernel(blocks, replicas, sections, subs, features_ref, tiles_ref, source_ref, held_ref, ring,
                  ring_send, ring_recv, give_send, give_recv, own_sem, held_sem):
    blk, rep = lax.axis_index("blk"), lax.axis_index("rep")
    share = features_ref.shape[0] // replicas
    sub = share // subs
    odd = lax.rem(blk, 2)
    position = (1 - odd) * lax.div(blk, 2) + odd * (blocks - 1 - lax.div(blk, 2))

    def block_at(offset):
        p = lax.rem(position + blocks + offset, blocks)
        back = lax.div(p, blocks // 2)
        return (1 - back) * (2 * p) + back * (2 * (blocks - 1 - p) + 1)

    def rows(who, h):
        return pl.ds(pl.multiple_of(who * share + h * sub, sub), sub)

    hops = blocks // 2
    ways = (1, -1)
    barrier = pltpu.get_barrier_semaphore()
    for way in ways:
        pl.semaphore_signal(barrier, inc=1, device_id=(block_at(way), rep), device_id_type=MESH)
    for d in range(1, replicas):
        pl.semaphore_signal(barrier, inc=1, device_id=(blk, lax.rem(rep + d, replicas)), device_id_type=MESH)
    pl.semaphore_wait(barrier, replicas + 1)

    def ring_copy(w, k, h):
        source = features_ref.at[rows(rep, h)] if k == 0 else ring.at[w, k - 1, h]
        return pltpu.make_async_remote_copy(
            src_ref=source, dst_ref=ring.at[w, k, h], send_sem=ring_send.at[w, k, h],
            recv_sem=ring_recv.at[w, k, h], device_id=(block_at(ways[w]), rep), device_id_type=MESH)

    def travels(w, k, h):
        return k < hops - 1 or (k == hops - 1 and h * 2 // subs == w)

    for h in range(subs):
        for w in range(2):
            if travels(w, 0, h):
                ring_copy(w, 0, h).start()
    held = pltpu.make_async_copy(tiles_ref, held_ref, held_sem)
    held.start()
    own = pltpu.make_async_copy(features_ref, source_ref.at[0], own_sem)

    @pl.when(rep == 0)
    def _():
        own.start()

    arrivals = [(k, h, w) for k in range(hops) for h in range(subs) for w in range(2) if travels(w, k, h)]

    def give(k, h, w):
        section = lax.rem(blk - block_at(-ways[w] * (k + 1)) + blocks, blocks)
        target, index = lax.div(section, sections), lax.rem(section, sections)
        place = source_ref.at[index, rows(rep, h)]
        here = pltpu.make_async_copy(ring.at[w, k, h], place, give_send.at[w, k, h])
        there = pltpu.make_async_remote_copy(
            src_ref=ring.at[w, k, h], dst_ref=place, send_sem=give_send.at[w, k, h],
            recv_sem=give_recv.at[index, rep, h], device_id=(blk, target), device_id_type=MESH)
        return target, here, there

    for k, h, w in arrivals:
        ring_copy(w, k, h).wait_recv()
        if travels(w, k + 1, h):
            ring_copy(w, k + 1, h).start()
        target, here, there = give(k, h, w)

        @pl.when(target == rep)
        def _():
            here.start()

        @pl.when(target != rep)
        def _():
            there.start()

    for k, h, w in arrivals:
        ring_copy(w, k, h).wait_send()
        target, here, there = give(k, h, w)

        @pl.when(target == rep)
        def _():
            here.wait()

        @pl.when(target != rep)
        def _():
            there.wait_send()

    @pl.when(rep == 0)
    def _():
        own.wait()

    held.wait()
    for index in range(sections):
        def arrive(index=index):
            for d in range(1, replicas):
                giver = lax.rem(rep + d, replicas)
                for h in range(subs):
                    pltpu.make_async_remote_copy(
                        src_ref=ring.at[0, 0, h], dst_ref=source_ref.at[index, rows(giver, h)],
                        send_sem=give_send.at[0, 0, h], recv_sem=give_recv.at[index, giver, h],
                        device_id=(blk, giver), device_id_type=MESH).wait_recv()

        if index == 0:
            pl.when(rep != 0)(arrive)
        else:
            arrive()


def gather_sources(features, tile_values, blocks, replicas):
    sections = tile_values.shape[1]
    rows, width = features.shape
    subs = 2 * largest_divisor(rows // replicas // 32, SUBS // 2)
    sub = rows // replicas // subs
    hops = blocks // 2
    vmem = pl.BlockSpec(memory_space=pltpu.VMEM)
    dma = pltpu.SemaphoreType.DMA
    return pl.pallas_call(
        functools.partial(gather_kernel, blocks, replicas, sections, subs),
        out_shape=(
            jax.ShapeDtypeStruct((sections, rows, width), features.dtype),
            jax.ShapeDtypeStruct(tile_values.shape, tile_values.dtype),
        ),
        in_specs=[vmem, pl.BlockSpec(memory_space=pl.ANY)],
        out_specs=(vmem, vmem),
        scratch_shapes=[
            pltpu.VMEM((2, hops, subs, sub, width), features.dtype),
            dma((2, hops, subs)), dma((2, hops, subs)), dma((2, hops, subs)),
            dma((sections, replicas, subs)), dma(()), dma(()),
        ],
        compiler_params=pltpu.CompilerParams(collective_id=1, has_side_effects=True, vmem_limit_bytes=2 * GRANT),
        cost_estimate=pl.CostEstimate(
            flops=0, bytes_accessed=96 * rows * width * features.dtype.itemsize, transcendentals=0
        ),
        name="gather_sources",
    )(features, tile_values)


def sections_kernel(find, group, place_ref, count_ref, source_ref, tiles_ref, acc_ref):
    step = pl.program_id(0)
    slots, tile = tiles_ref.shape[2], tiles_ref.shape[3]
    row_tiles = source_ref.shape[1] // tile
    section, chunk, active = find(step, count_ref)
    count = count_ref[0, section]
    base = chunk * slots

    @pl.when(step == 0)
    def _():
        acc_ref[...] = jnp.zeros_like(acc_ref)

    def body(g, carry):
        for u in range(group):
            k = g * group + u
            place = place_ref[0, section, base + k]
            column, target = lax.rem(place, row_tiles), lax.div(place, row_tiles)
            piece = source_ref[section, pl.ds(pl.multiple_of(column * tile, tile), tile), :]
            product = jnp.dot(tiles_ref[0, 0, k], piece, preferred_element_type=jnp.float32)
            rows = pl.ds(pl.multiple_of(target * tile, tile), tile)
            acc_ref[rows, :] += jnp.where(base + k < count, product, 0.0)
        return carry

    live = jnp.where(active, jnp.clip(count - base, 0, slots), 0)
    lax.fori_loop(0, (live + group - 1) // group, body, 0)


def section_sums(sources, tile_values, tile_place, tile_count):
    sections, slots, tile = tile_values.shape[1:4]
    rows, width = sources.shape[1:]
    block = largest_divisor(slots, BLOCK)
    group = largest_divisor(block, GROUP)

    def find(step, count_ref):
        section, chunk = jnp.int32(0), jnp.int32(0)
        start, active = jnp.int32(0), False
        for s in range(sections):
            steps = lax.div(count_ref[0, s] + block - 1, block)
            inside = step >= start
            section = jnp.where(inside, s, section)
            chunk = jnp.where(inside, jnp.minimum(step - start, steps - 1), chunk)
            start = start + steps
        return section, chunk, step < start

    def tiles_map(step, place_ref, count_ref):
        section, chunk, _ = find(step, count_ref)
        return (0, section, chunk, 0, 0)

    vmem = pl.BlockSpec(memory_space=pltpu.VMEM)
    return pl.pallas_call(
        functools.partial(sections_kernel, find, group),
        out_shape=jax.ShapeDtypeStruct((rows, width), jnp.float32),
        grid_spec=pltpu.PrefetchScalarGridSpec(
            num_scalar_prefetch=2, grid=(sections * slots // block,),
            in_specs=[vmem, pl.BlockSpec((1, 1, block, tile, tile), tiles_map)], out_specs=vmem
        ),
        compiler_params=pltpu.CompilerParams(vmem_limit_bytes=GRANT),
        name="section_sums",
    )(tile_place, tile_count, sources, tile_values)


def reduce_kernel(chips, chunks, part_ref, agg_ref, core_in, send_buf, recv_buf,
                  s1, r1, s2, r2, s3, r3, s4, r4):
    blk, rep = lax.axis_index("blk"), lax.axis_index("rep")
    core, chip = lax.rem(rep, 2), lax.div(rep, 2)
    rows = part_ref.shape[0]
    half = rows // 2
    size = half // chips // chunks
    other = chip * 2 + (1 - core)

    def peer(d):
        return lax.rem(chip + d, chips)

    def local(piece, ch):
        return pl.ds(pl.multiple_of((piece * chunks + ch) * size, size), size)

    def place(which, piece, ch):
        return pl.ds(pl.multiple_of(which * half + (piece * chunks + ch) * size, size), size)

    barrier = pltpu.get_barrier_semaphore()
    pl.semaphore_signal(barrier, inc=1, device_id=(blk, other), device_id_type=MESH)
    for d in range(1, chips):
        pl.semaphore_signal(barrier, inc=1, device_id=(blk, peer(d) * 2 + core), device_id_type=MESH)
    pl.semaphore_wait(barrier, chips)

    order = [(ch, d) for ch in range(chunks) for d in list(range(1, chips)) + [0]]
    stage1, stage2, stage3, stage4 = {}, {}, {}, {}
    for ch, d in order:
        copy = pltpu.make_async_remote_copy(
            src_ref=part_ref.at[place(1 - core, peer(d), ch)], dst_ref=core_in.at[local(peer(d), ch)],
            send_sem=s1.at[d, ch], recv_sem=r1.at[d, ch], device_id=(blk, other), device_id_type=MESH)
        copy.start()
        stage1[ch, d] = copy
    for ch, d in order:
        if d == 0:
            continue
        stage1[ch, d].wait_recv()
        total = part_ref[place(core, peer(d), ch), :] + core_in[local(peer(d), ch), :]
        send_buf[d - 1, ch] = total.astype(jnp.bfloat16)
        copy = pltpu.make_async_remote_copy(
            src_ref=send_buf.at[d - 1, ch], dst_ref=recv_buf.at[d - 1, ch],
            send_sem=s2.at[d, ch], recv_sem=r2.at[d, ch],
            device_id=(blk, peer(d) * 2 + core), device_id_type=MESH)
        copy.start()
        stage2[ch, d] = copy
    for ch in range(chunks):
        stage1[ch, 0].wait_recv()
        total = part_ref[place(core, chip, ch), :] + core_in[local(chip, ch), :]
        for d in range(1, chips):
            stage2[ch, d].wait_recv()
            total = total + recv_buf[d - 1, ch].astype(jnp.float32)
        mine = place(core, chip, ch)
        agg_ref[mine, :] = total.astype(jnp.bfloat16)
        for d in list(range(1, chips)) + [0]:
            target = other if d == 0 else peer(d) * 2 + core
            copy = pltpu.make_async_remote_copy(
                src_ref=agg_ref.at[mine], dst_ref=agg_ref.at[mine],
                send_sem=s3.at[d, ch], recv_sem=r3.at[d, ch],
                device_id=(blk, target), device_id_type=MESH)
            copy.start()
            stage3[ch, d] = copy
    for ch in range(chunks):
        for d in range(1, chips):
            stage3[ch, d].wait_recv()
            came = place(core, lax.rem(chip + chips - d, chips), ch)
            copy = pltpu.make_async_remote_copy(
                src_ref=agg_ref.at[came], dst_ref=agg_ref.at[came],
                send_sem=s4.at[d, ch], recv_sem=r4.at[d, ch],
                device_id=(blk, other), device_id_type=MESH)
            copy.start()
            stage4[ch, d] = copy
    for ch, d in order:
        stage1[ch, d].wait_send()
        stage3[ch, d].wait_send()
        if d == 0:
            stage3[ch, d].wait_recv()
        else:
            stage2[ch, d].wait_send()
            stage4[ch, d].wait()


def replica_sum(part, replicas):
    rows, width = part.shape
    chips = replicas // 2
    chunks = largest_divisor(rows // 2 // chips // 16, CHUNKS)
    size = rows // 2 // chips // chunks
    dma = pltpu.SemaphoreType.DMA((chips, chunks))
    vmem = pl.BlockSpec(memory_space=pltpu.VMEM)
    return pl.pallas_call(
        functools.partial(reduce_kernel, chips, chunks),
        out_shape=jax.ShapeDtypeStruct((rows, width), jnp.bfloat16),
        in_specs=[vmem],
        out_specs=vmem,
        scratch_shapes=[
            pltpu.VMEM((rows // 2, width), jnp.float32),
            pltpu.VMEM((chips - 1, chunks, size, width), jnp.bfloat16),
            pltpu.VMEM((chips - 1, chunks, size, width), jnp.bfloat16),
        ] + [dma] * 8,
        compiler_params=pltpu.CompilerParams(collective_id=0, has_side_effects=True, vmem_limit_bytes=GRANT),
        name="replica_sum",
    )(part)


def activate_kernel(agg_ref, weight_ref, bias_ref, out_ref):
    output = jnp.dot(agg_ref[...], weight_ref[...], preferred_element_type=jnp.float32) + bias_ref[...]
    out_ref[...] = jnp.maximum(output, 0.0).astype(out_ref.dtype)


def activate(aggregated, weight, bias):
    rows, width = aggregated.shape
    hidden = weight.shape[1]
    step = largest_divisor(rows, ROWS_STEP)
    return pl.pallas_call(
        activate_kernel,
        out_shape=jax.ShapeDtypeStruct((rows, hidden), jnp.bfloat16),
        grid=(rows // step,),
        in_specs=[
            pl.BlockSpec((step, width), lambda i: (i, 0)),
            pl.BlockSpec((width, hidden), lambda i: (0, 0)),
            pl.BlockSpec((1, hidden), lambda i: (0, 0)),
        ],
        out_specs=pl.BlockSpec((step, hidden), lambda i: (i, 0)),
        compiler_params=pltpu.CompilerParams(vmem_limit_bytes=GRANT),
        name="activate",
    )(aggregated, weight, bias[None, :])


def shards(blocks, replicas, features, weight, bias, tile_values, tile_place, tile_count):
    sources, held = gather_sources(features, tile_values, blocks, replicas)
    part = section_sums(sources, held, tile_place, tile_count)
    aggregated = replica_sum(part, replicas)
    return activate(aggregated, weight, bias)


def solution(mesh):
    in_specs = (
        P("blk", None),
        P(),
        P(),
        P("blk", "rep", None, None, None),
        P("blk", "rep", None),
        P("blk", "rep"),
    )
    body = functools.partial(shards, mesh.shape["blk"], mesh.shape["rep"])
    return jax.shard_map(body, mesh=mesh, in_specs=in_specs, out_specs=P("blk", None), check_vma=False)
```
